32 devices in a mesh: leaf: 4 (over z), inner: 8 (over y, x, core).
Axes of the slice: x: 2, y: 2, z: 4, core: 2. Of those that a mesh axis runs over, the one named last changes fastest.
Arguments:
- sources: bfloat16 [16384, 640], P(('leaf', 'inner')), may hold values from -6 to 6
- leaf_perm: int32 [32, 512], P(('leaf', 'inner')), may hold values from 0 to 511, each once within a row
- leaf_factor: bfloat16 [16384, 512], P(('leaf', 'inner')), may hold values from -0.25 to 0.25
- owner_map: int32 [2, 4096], P(None, 'inner'), may hold values from 0 to 1
- coupling: float32 [2, 16384], P(None, ('leaf', 'inner')), may hold values from -0.8 to 0.8
- transfer: bfloat16 [3, 2, 16384, 512], P(None, None, ('leaf', 'inner')), may hold values from -0.1875 to 0.1875
Outputs:
- targets: bfloat16 [16384, 640], P(('leaf', 'inner'))
The draws below stay inside these ranges and needn't reach their ends.
Inputs may be any that keep to these rules, and one draw needn't show every extreme that they name: Each row of leaf_perm names every number of 0 to 511 once.
All inputs are finite; a program needn't handle non-finite values.
Results may differ from the reference program's by a relative error of at most 0.007.
Values may be sent and summed in bfloat16 or wider, within the bound.
A program may use at most 64 MiB of HBM per device.

```python
import jax
import jax.numpy as jnp
from jax import lax

B = 512
RHS = 320
LEVELS = 3
HALF = 256
PAIRS = 2
BLOCKS = 32
INNER_ROWS = 4096
UNKNOWNS = 16384
N_LEAF = 4
N_INNER = 8


def with_ends(drawn, stream_key, smallest, top_value):
    extent = drawn.shape
    index_at = [jax.random.randint(jax.random.fold_in(stream_key, axis), (), 0, extent[axis]) for axis in range(len(extent))]
    drawn = drawn.at[tuple(index_at)].set(smallest)
    longest = extent.index(max(extent))
    index_at[longest] = (index_at[longest] + 1) % extent[longest]
    return drawn.at[tuple(index_at)].set(top_value)


def block_levels(key, shape, split, low, largest):
    def one(axis_at, blocks):
        steps = jax.random.uniform(jax.random.fold_in(jax.random.fold_in(key, 6), axis_at), (blocks,), jnp.float32, low / len(split), largest / len(split))
        return jnp.repeat(jnp.exp(steps), shape[axis_at] // blocks).reshape((-1,) + (1,) * (len(shape) - axis_at - 1))

    gain = one(*split[0])
    for cut in split[1:]:
        gain = gain * one(*cut)
    return gain


def bell_draw(key, dims, spread, bound, split=(), held_as=jnp.bfloat16):
    values = jax.random.normal(key, dims, jnp.float32) * spread
    if len(split) > 0:
        values = block_levels(key, dims, split, -0.22, 0.18) * values
    return jnp.clip(values, min=-bound, max=bound).astype(held_as)


def setup_inputs(seed: int = 0) -> dict:
    arg_keys = jax.random.split(jax.random.key(seed), 7)
    sources = bell_draw(arg_keys[0], (UNKNOWNS, 2 * RHS), 1.0, 6.0, ((0, 32),))
    leaf_perm = jax.vmap(lambda own: jax.random.permutation(own, B))(jax.random.split(arg_keys[1], BLOCKS)).reshape((BLOCKS, B)).astype(jnp.int32)
    leaf_factor = bell_draw(arg_keys[2], (UNKNOWNS, B), B ** -0.5, 0.25, ((0, 32),))
    owner_map = with_ends(jax.random.randint(arg_keys[3], (PAIRS, INNER_ROWS), 0, 2), jax.random.fold_in(arg_keys[3], 1), 0, 1).astype(jnp.int32)
    coupling = jnp.clip(jax.random.uniform(arg_keys[4], (2, UNKNOWNS), jnp.float32, -0.8, 0.8) * block_levels(arg_keys[4], (2, UNKNOWNS), ((1, 32),), -0.4, 0.0), -0.8, 0.8)
    transfer = bell_draw(arg_keys[5], (LEVELS, 2, UNKNOWNS, B), (2 * B) ** -0.5, 0.1875, ((2, 32),))
    return {"sources": sources, "leaf_perm": leaf_perm, "leaf_factor": leaf_factor, "owner_map": owner_map, "coupling": coupling, "transfer": transfer}


def complex_apply(weights, columns):
    real_part = jnp.dot(weights[0], columns, preferred_element_type=jnp.float32)
    imag_part = jnp.dot(weights[1], columns, preferred_element_type=jnp.float32)
    column_half = columns.shape[1] // 2
    return jnp.concatenate([real_part[:, :column_half] - imag_part[:, column_half:], real_part[:, column_half:] + imag_part[:, :column_half]], axis=1)


def precondition(pieces):
    factor, source_rows = pieces
    height = factor.shape[0]
    row_iota = lax.broadcasted_iota(jnp.int32, (height, height), 0)
    col_iota = lax.broadcasted_iota(jnp.int32, (height, height), 1)
    real_lower = jnp.where(row_iota >= col_iota, factor, jnp.zeros_like(factor))
    imag_lower = jnp.where(row_iota > col_iota, factor.T, jnp.zeros_like(factor))
    lower = jnp.stack([real_lower, imag_lower])
    return (source_rows.astype(jnp.float32) + complex_apply(lower, source_rows)).astype(jnp.bfloat16)


def level_apply(pieces):
    return complex_apply(pieces[0], pieces[1]).astype(jnp.bfloat16)


def reference(sources, leaf_perm, leaf_factor, owner_map, coupling, transfer):
    blocks = N_LEAF * N_INNER
    columns = 2 * RHS
    panels = sources.reshape(blocks, B, columns)
    panels = jnp.take_along_axis(panels, leaf_perm[:, :, None], axis=1)
    factors = leaf_factor.reshape(blocks, B, B)
    prepared = lax.map(precondition, (factors, panels))
    paired = prepared.reshape(PAIRS, 2, N_INNER, B, columns)
    owner_rows = (owner_map.reshape(PAIRS, N_INNER, B) == 0)[:, :, :, None]
    first_part = jnp.where(owner_rows, paired[:, 0], paired[:, 1]).astype(jnp.float32)[:, None]
    other_part = jnp.where(owner_rows, paired[:, 1], paired[:, 0]).astype(jnp.float32)[:, None]
    couple = coupling.reshape(2, PAIRS, 2, N_INNER, B, 1)
    mixed_real = first_part[..., :RHS] + couple[0] * other_part[..., :RHS] - couple[1] * other_part[..., RHS:]
    mixed_imag = first_part[..., RHS:] + couple[0] * other_part[..., RHS:] + couple[1] * other_part[..., :RHS]
    field_now = jnp.concatenate([mixed_real, mixed_imag], axis=-1).astype(jnp.bfloat16)
    field_now = field_now.reshape(N_LEAF, N_INNER, B, columns)
    for section_number in range(LEVELS):
        distance = N_INNER >> (section_number + 1)
        grouped = field_now.reshape(N_LEAF, N_INNER // (2 * distance), 2, distance, B, columns)
        lower_side = grouped[:, :, 0]
        upper_side = grouped[:, :, 1]
        top_rows = jnp.concatenate([lower_side[..., :HALF, :], upper_side[..., :HALF, :]], axis=-2)
        bottom_rows = jnp.concatenate([lower_side[..., HALF:, :], upper_side[..., HALF:, :]], axis=-2)
        joined = jnp.stack([top_rows, bottom_rows], axis=2).reshape(blocks, B, columns)
        weights = jnp.moveaxis(transfer[section_number].reshape(2, blocks, B, B), 1, 0)
        field_now = lax.map(level_apply, (weights, joined)).reshape(N_LEAF, N_INNER, B, columns)
    return field_now.reshape(UNKNOWNS, columns)
```

```python
import functools

import jax
import jax.numpy as jnp
from jax import lax
from jax.experimental import pallas as pl
from jax.experimental.pallas import tpu as pltpu
from jax.sharding import PartitionSpec as P

LANES = 128
PIECE = LANES // 2
MESH = pl.DeviceIdType.MESH
F32 = jnp.float32
BF16 = jnp.bfloat16


def dot(a, b):
    return jnp.dot(a, b, preferred_element_type=F32)


def as_column(row):
    return jnp.broadcast_to(row, (LANES, row.shape[1])).T


def kernel(
    levels,
    perm_ref,
    owner_ref,
    couple_ref,
    source_hbm,
    factor_hbm,
    transfer_hbm,
    out_ref,
    source,
    factor,
    weights,
    lower_real,
    lower_imag,
    mine,
    prepared,
    theirs,
    inputs,
    outgoing,
    final,
    partner_couple,
    partner_owner,
    load_sem,
    small_send,
    small_recv,
    side_send,
    side_recv,
    sib_send,
    sib_recv,
    level_send,
    level_recv,
):
    height, width = source.shape
    half = height // 2
    pieces = width // LANES
    leaf = lax.axis_index("leaf")
    inner = lax.axis_index("inner")
    inner_size = lax.axis_size("inner")
    sibling = leaf + 1 - 2 * lax.rem(leaf, 2)
    which_side = lax.rem(leaf, 2)
    pair = leaf // 2

    bits, partners = [], []
    for level in range(levels):
        distance = inner_size >> (level + 1)
        bit = lax.rem(inner // distance, 2)
        bits.append(bit)
        partners.append(inner + distance - 2 * distance * bit)

    def rows_at(flag):
        return pl.ds(pl.multiple_of(flag * half, half), half)

    loads = [
        pltpu.make_async_copy(source_hbm, source, load_sem.at[0]),
        pltpu.make_async_copy(factor_hbm, factor, load_sem.at[1]),
    ]
    for level in range(levels):
        loads.append(
            pltpu.make_async_copy(
                transfer_hbm.at[level], weights.at[level], load_sem.at[2 + level]
            )
        )
    for load in loads:
        load.start()

    barrier = pltpu.get_barrier_semaphore()
    pl.semaphore_signal(barrier, inc=1, device_id={"leaf": sibling}, device_id_type=MESH)
    for level in range(levels):
        pl.semaphore_signal(
            barrier, inc=1, device_id={"inner": partners[level]}, device_id_type=MESH
        )

    lane = lax.broadcasted_iota(jnp.int32, (height, LANES), 1)
    low_lanes = lane < PIECE
    sign_even = jnp.where(low_lanes, -1.0, 1.0).astype(F32)

    def turned(value, piece):
        rolled = pltpu.roll(value, PIECE, 1)
        sign = sign_even[: value.shape[0]]
        return rolled * sign if piece % 2 == 0 else rolled * -sign

    perm_column = as_column(perm_ref[...])
    one_hot = jnp.concatenate(
        [
            jnp.where(perm_column == lane + LANES * tile, 1.0, 0.0).astype(BF16)
            for tile in range(height // LANES)
        ],
        axis=1,
    )

    loads[1].wait()
    row_half = lax.broadcasted_iota(jnp.int32, (half, half), 0)
    col_half = lax.broadcasted_iota(jnp.int32, (half, half), 1)
    for part in range(2):
        here = slice(part * half, (part + 1) * half)
        block = factor[here, here].astype(F32)
        lower_real[here, here] = jnp.where(row_half >= col_half, block, 0.0).astype(BF16)
        lower_imag[here, here] = jnp.where(row_half > col_half, block.T, 0.0).astype(BF16)
    lower_real[half:, :half] = factor[half:, :half]
    lower_imag[half:, :half] = factor[:half, half:].astype(F32).T.astype(BF16)

    loads[0].wait()
    pl.semaphore_wait(barrier, levels + 1)

    small = [
        pltpu.make_async_remote_copy(
            src_ref=couple_ref,
            dst_ref=partner_couple,
            send_sem=small_send.at[0],
            recv_sem=small_recv.at[0],
            device_id={"inner": partners[0]},
            device_id_type=MESH,
        ),
        pltpu.make_async_remote_copy(
            src_ref=owner_ref,
            dst_ref=partner_owner,
            send_sem=small_send.at[1],
            recv_sem=small_recv.at[1],
            device_id={"inner": partners[0]},
            device_id_type=MESH,
        ),
    ]
    for copy in small:
        copy.start()

    kept, other = rows_at(bits[0]), rows_at(1 - bits[0])

    def side_copy(piece):
        return pltpu.make_async_remote_copy(
            src_ref=mine.at[piece],
            dst_ref=prepared.at[piece, kept],
            send_sem=side_send.at[piece],
            recv_sem=side_recv.at[piece],
            device_id={"inner": partners[0]},
            device_id_type=MESH,
        )

    def sibling_copy(piece, stage):
        rows = kept if stage == 0 else other
        return pltpu.make_async_remote_copy(
            src_ref=prepared.at[piece, rows],
            dst_ref=theirs.at[piece, rows],
            send_sem=sib_send.at[stage, piece],
            recv_sem=sib_recv.at[stage, piece],
            device_id={"leaf": sibling},
            device_id_type=MESH,
        )

    def level_copy(level, piece):
        return pltpu.make_async_remote_copy(
            src_ref=outgoing.at[level - 1, piece],
            dst_ref=inputs.at[level, piece, rows_at(bits[level])],
            send_sem=level_send.at[level - 1, piece],
            recv_sem=level_recv.at[level - 1, piece],
            device_id={"inner": partners[level]},
            device_id_type=MESH,
        )

    def prepare(piece):
        real_tile, imag_tile = piece // 2, (pieces + piece) // 2
        low_tile, high_tile = (
            (real_tile, imag_tile) if piece % 2 == 0 else (imag_tile, real_tile)
        )
        column = jnp.where(
            low_lanes,
            source[:, low_tile * LANES : (low_tile + 1) * LANES].astype(F32),
            source[:, high_tile * LANES : (high_tile + 1) * LANES].astype(F32),
        ).astype(BF16)
        permuted = dot(one_hot, column)
        permuted_half = permuted.astype(BF16)
        results = []
        for part in range(2):
            here = slice(part * half, (part + 1) * half)
            depth = (part + 1) * half
            real_part = dot(lower_real[here, :depth], permuted_half[:depth])
            imag_part = dot(lower_imag[here, :depth], permuted_half[:depth])
            results.append(
                (permuted[here] + real_part + turned(imag_part, piece)).astype(BF16)
            )
        top, bottom = results
        upper = bits[0] == 1
        prepared[piece, kept, :] = jnp.where(upper, bottom, top)
        mine[piece] = jnp.where(upper, top, bottom)
        sibling_copy(piece, 0).start()
        side_copy(piece).start()

    def forward(piece):
        side_copy(piece).wait_recv()
        sibling_copy(piece, 1).start()

    lag = 2
    for piece in range(pieces):
        prepare(piece)
        if piece >= lag:
            forward(piece - lag)

    for copy in small:
        copy.wait_recv()

    def in_input_order(own, partner):
        low, high = slice(0, half), slice(half, height)
        return jnp.concatenate(
            [
                jnp.where(bits[0] == 0, own[:, low], partner[:, high]),
                jnp.where(bits[0] == 1, own[:, high], partner[:, low]),
            ],
            axis=1,
        )

    couple_rows = in_input_order(couple_ref[...], partner_couple[...])
    owner_rows = in_input_order(
        owner_ref[pl.ds(pair, 1), :], partner_owner[pl.ds(pair, 1), :]
    )
    couple_real = as_column(couple_rows[0:1])
    couple_imag = as_column(couple_rows[1:2])
    own_first = as_column(owner_rows) == which_side

    for piece in range(pieces - lag, pieces):
        forward(piece)

    def combine(piece):
        sibling_copy(piece, 0).wait_recv()
        sibling_copy(piece, 1).wait_recv()
        here = prepared[piece].astype(F32)
        there = theirs[piece].astype(F32)
        first_part = jnp.where(own_first, here, there)
        other_part = jnp.where(own_first, there, here)
        return (
            first_part + couple_real * other_part + couple_imag * turned(other_part, piece)
        ).astype(BF16)

    def rows_of(level, piece, rows, field):
        real_part = dot(weights[level, 0, rows, :], field)
        imag_part = dot(weights[level, 1, rows, :], field)
        return (real_part + turned(imag_part, piece)).astype(BF16)

    loaded = set()

    def run_level(level, piece):
        if level == 0:
            field = combine(piece)
        else:
            level_copy(level, piece).wait_recv()
            field = inputs[level, piece]
        if level not in loaded:
            loads[2 + level].wait()
            loaded.add(level)
        if level + 1 < levels:
            bit = bits[level + 1]
            outgoing[level, piece] = rows_of(level, piece, rows_at(1 - bit), field)
            level_copy(level + 1, piece).start()
            inputs[level + 1, piece, rows_at(bit), :] = rows_of(
                level, piece, rows_at(bit), field
            )
        else:
            final[piece] = rows_of(level, piece, slice(None), field)

    for step in range(pieces + levels - 1):
        for level in range(levels):
            piece = step - level
            if 0 <= piece < pieces:
                run_level(level, piece)

    for tile in range(pieces):
        low_piece, high_piece = [
            place if place < pieces else place - pieces for place in (2 * tile, 2 * tile + 1)
        ]
        out_ref[:, tile * LANES : (tile + 1) * LANES] = jnp.where(
            low_lanes, final[low_piece].astype(F32), final[high_piece].astype(F32)
        ).astype(BF16)

    for copy in small:
        copy.wait_send()
    for piece in range(pieces):
        side_copy(piece).wait_send()
        sibling_copy(piece, 0).wait_send()
        sibling_copy(piece, 1).wait_send()
        for level in range(1, levels):
            level_copy(level, piece).wait_send()


def body(sources, leaf_perm, leaf_factor, owner_map, coupling, transfer):
    height, width = sources.shape
    half = height // 2
    levels = transfer.shape[0]
    pieces = width // LANES
    assert width == pieces * LANES and pieces % 2 == 1
    vmem = pl.BlockSpec(memory_space=pltpu.VMEM)
    anywhere = pl.BlockSpec(memory_space=pl.ANY)
    dma = pltpu.SemaphoreType.DMA
    return pl.pallas_call(
        functools.partial(kernel, levels),
        out_shape=jax.ShapeDtypeStruct(sources.shape, sources.dtype),
        in_specs=[vmem, vmem, vmem, anywhere, anywhere, anywhere],
        out_specs=vmem,
        scratch_shapes=[
            pltpu.VMEM(sources.shape, BF16),
            pltpu.VMEM(leaf_factor.shape, BF16),
            pltpu.VMEM(transfer.shape, BF16),
            pltpu.VMEM(leaf_factor.shape, BF16),
            pltpu.VMEM(leaf_factor.shape, BF16),
            pltpu.VMEM((pieces, half, LANES), BF16),
            pltpu.VMEM((pieces, height, LANES), BF16),
            pltpu.VMEM((pieces, height, LANES), BF16),
            pltpu.VMEM((levels, pieces, height, LANES), BF16),
            pltpu.VMEM((levels - 1, pieces, half, LANES), BF16),
            pltpu.VMEM((pieces, height, LANES), BF16),
            pltpu.VMEM(coupling.shape, coupling.dtype),
            pltpu.VMEM(owner_map.shape, owner_map.dtype),
            dma((2 + levels,)),
            dma((2,)),
            dma((2,)),
            dma((pieces,)),
            dma((pieces,)),
            dma((2, pieces)),
            dma((2, pieces)),
            dma((levels - 1, pieces)),
            dma((levels - 1, pieces)),
        ],
        compiler_params=pltpu.CompilerParams(collective_id=0, has_side_effects=True, vmem_limit_bytes=58 * 1024 * 1024),
        name="apply",
    )(leaf_perm, owner_map, coupling, sources, leaf_factor, transfer)


def solution(mesh):
    placed = (
        P(("leaf", "inner"), None),
        P(("leaf", "inner"), None),
        P(("leaf", "inner"), None),
        P(None, "inner"),
        P(None, ("leaf", "inner")),
        P(None, None, ("leaf", "inner"), None),
    )
    return jax.shard_map(
        body, mesh=mesh, in_specs=placed, out_specs=P(("leaf", "inner"), None), check_vma=False
    )
```

```python
import functools

import jax
import jax.numpy as jnp
from jax import lax
from jax.experimental import pallas as pl
from jax.experimental.pallas import tpu as pltpu
from jax.sharding import PartitionSpec as P

LANES = 128
PIECE = LANES // 2
MESH = pl.DeviceIdType.MESH
F32 = jnp.float32
BF16 = jnp.bfloat16


def dot(a, b):
    return jnp.dot(a, b, preferred_element_type=F32)


def as_column(row):
    return jnp.broadcast_to(row, (LANES, row.shape[1])).T


def kernel(
    levels,
    perm_hbm,
    owner_hbm,
    couple_hbm,
    source_hbm,
    factor_hbm,
    transfer_hbm,
    out_ref,
    perm_ref,
    owner_ref,
    couple_ref,
    source,
    factor,
    weights,
    lower_real,
    lower_imag,
    mine,
    prepared,
    theirs,
    inputs,
    outgoing,
    final,
    partner_couple,
    partner_owner,
    load_sem,
    small_send,
    small_recv,
    side_send,
    side_recv,
    sib_send,
    sib_recv,
    level_send,
    level_recv,
):
    height, width = source.shape
    half = height // 2
    pieces = width // LANES
    leaf = lax.axis_index("leaf")
    inner = lax.axis_index("inner")
    inner_size = lax.axis_size("inner")
    sibling = leaf + 1 - 2 * lax.rem(leaf, 2)
    which_side = lax.rem(leaf, 2)
    pair = leaf // 2

    bits, partners = [], []
    for level in range(levels):
        distance = inner_size >> (level + 1)
        bit = lax.rem(inner // distance, 2)
        bits.append(bit)
        partners.append(inner + distance - 2 * distance * bit)

    def rows_at(flag):
        return pl.ds(pl.multiple_of(flag * half, half), half)

    barrier = pltpu.get_barrier_semaphore()
    pl.semaphore_signal(barrier, inc=1, device_id={"leaf": sibling}, device_id_type=MESH)
    for level in range(levels):
        pl.semaphore_signal(
            barrier, inc=1, device_id={"inner": partners[level]}, device_id_type=MESH
        )

    load_list = [
        (perm_hbm, perm_ref),
        (source_hbm, source),
        (factor_hbm, factor),
        (couple_hbm, couple_ref),
        (owner_hbm, owner_ref),
    ] + [(transfer_hbm.at[level], weights.at[level]) for level in range(levels)]
    loads = [
        pltpu.make_async_copy(origin, place, load_sem.at[number])
        for number, (origin, place) in enumerate(load_list)
    ]
    for load in loads:
        load.start()

    lane = lax.broadcasted_iota(jnp.int32, (height, LANES), 1)
    low_lanes = lane < PIECE
    sign_even = jnp.where(low_lanes, -1.0, 1.0).astype(F32)

    def turned(value, piece):
        rolled = pltpu.roll(value, PIECE, 1)
        sign = sign_even[: value.shape[0]]
        return rolled * sign if piece % 2 == 0 else rolled * -sign

    loads[0].wait()
    perm_column = as_column(perm_ref[...])
    one_hot = jnp.concatenate(
        [
            jnp.where(perm_column == lane + LANES * tile, 1.0, 0.0).astype(BF16)
            for tile in range(height // LANES)
        ],
        axis=1,
    )

    loads[2].wait()
    row_half = lax.broadcasted_iota(jnp.int32, (half, half), 0)
    col_half = lax.broadcasted_iota(jnp.int32, (half, half), 1)
    for part in range(2):
        here = slice(part * half, (part + 1) * half)
        block = factor[here, here].astype(F32)
        lower_real[here, here] = jnp.where(row_half >= col_half, block, 0.0).astype(BF16)
        lower_imag[here, here] = jnp.where(row_half > col_half, block.T, 0.0).astype(BF16)
    lower_real[half:, :half] = factor[half:, :half]
    lower_imag[half:, :half] = factor[:half, half:].astype(F32).T.astype(BF16)

    loads[1].wait()
    loads[3].wait()
    loads[4].wait()

    small = [
        pltpu.make_async_remote_copy(
            src_ref=couple_ref,
            dst_ref=partner_couple,
            send_sem=small_send.at[0],
            recv_sem=small_recv.at[0],
            device_id={"inner": partners[0]},
            device_id_type=MESH,
        ),
        pltpu.make_async_remote_copy(
            src_ref=owner_ref,
            dst_ref=partner_owner,
            send_sem=small_send.at[1],
            recv_sem=small_recv.at[1],
            device_id={"inner": partners[0]},
            device_id_type=MESH,
        ),
    ]
    kept, other = rows_at(bits[0]), rows_at(1 - bits[0])

    def side_copy(piece):
        return pltpu.make_async_remote_copy(
            src_ref=mine.at[piece],
            dst_ref=prepared.at[piece, kept],
            send_sem=side_send.at[piece],
            recv_sem=side_recv.at[piece],
            device_id={"inner": partners[0]},
            device_id_type=MESH,
        )

    def sibling_copy(piece, stage):
        rows = kept if stage == 0 else other
        return pltpu.make_async_remote_copy(
            src_ref=prepared.at[piece, rows],
            dst_ref=theirs.at[piece, rows],
            send_sem=sib_send.at[stage, piece],
            recv_sem=sib_recv.at[stage, piece],
            device_id={"leaf": sibling},
            device_id_type=MESH,
        )

    def level_copy(level, piece):
        return pltpu.make_async_remote_copy(
            src_ref=outgoing.at[level - 1, piece],
            dst_ref=inputs.at[level, piece, rows_at(bits[level])],
            send_sem=level_send.at[level - 1, piece],
            recv_sem=level_recv.at[level - 1, piece],
            device_id={"inner": partners[level]},
            device_id_type=MESH,
        )

    def prepare(piece):
        real_tile, imag_tile = piece // 2, (pieces + piece) // 2
        low_tile, high_tile = (
            (real_tile, imag_tile) if piece % 2 == 0 else (imag_tile, real_tile)
        )
        column = jnp.where(
            low_lanes,
            source[:, low_tile * LANES : (low_tile + 1) * LANES].astype(F32),
            source[:, high_tile * LANES : (high_tile + 1) * LANES].astype(F32),
        ).astype(BF16)
        permuted = dot(one_hot, column)
        permuted_half = permuted.astype(BF16)
        results = []
        for part in range(2):
            here = slice(part * half, (part + 1) * half)
            depth = (part + 1) * half
            real_part = dot(lower_real[here, :depth], permuted_half[:depth])
            imag_part = dot(lower_imag[here, :depth], permuted_half[:depth])
            results.append(
                (permuted[here] + real_part + turned(imag_part, piece)).astype(BF16)
            )
        top, bottom = results
        upper = bits[0] == 1
        prepared[piece, kept, :] = jnp.where(upper, bottom, top)
        mine[piece] = jnp.where(upper, top, bottom)
        if piece == 0:
            pl.semaphore_wait(barrier, levels + 1)
        sibling_copy(piece, 0).start()
        side_copy(piece).start()
        if piece == 0:
            for copy in small:
                copy.start()

    def forward(piece):
        side_copy(piece).wait_recv()
        sibling_copy(piece, 1).start()

    lag = 2
    for piece in range(pieces):
        prepare(piece)
        if piece >= lag:
            forward(piece - lag)

    for copy in small:
        copy.wait_recv()

    def in_input_order(own, partner):
        low, high = slice(0, half), slice(half, height)
        return jnp.concatenate(
            [
                jnp.where(bits[0] == 0, own[:, low], partner[:, high]),
                jnp.where(bits[0] == 1, own[:, high], partner[:, low]),
            ],
            axis=1,
        )

    couple_rows = in_input_order(couple_ref[...], partner_couple[...])
    owner_rows = in_input_order(
        owner_ref[pl.ds(pair, 1), :], partner_owner[pl.ds(pair, 1), :]
    )
    couple_real = as_column(couple_rows[0:1])
    couple_imag = as_column(couple_rows[1:2])
    own_first = as_column(owner_rows) == which_side

    for piece in range(pieces - lag, pieces):
        forward(piece)

    def combine(piece):
        sibling_copy(piece, 0).wait_recv()
        sibling_copy(piece, 1).wait_recv()
        here = prepared[piece].astype(F32)
        there = theirs[piece].astype(F32)
        first_part = jnp.where(own_first, here, there)
        other_part = jnp.where(own_first, there, here)
        return (
            first_part + couple_real * other_part + couple_imag * turned(other_part, piece)
        ).astype(BF16)

    def rows_of(level, piece, rows, field):
        real_part = dot(weights[level, 0, rows, :], field)
        imag_part = dot(weights[level, 1, rows, :], field)
        return (real_part + turned(imag_part, piece)).astype(BF16)

    loaded = set()

    def run_level(level, piece):
        if level == 0:
            field = combine(piece)
        else:
            level_copy(level, piece).wait_recv()
            field = inputs[level, piece]
        if level not in loaded:
            loads[5 + level].wait()
            loaded.add(level)
        if level + 1 < levels:
            bit = bits[level + 1]
            outgoing[level, piece] = rows_of(level, piece, rows_at(1 - bit), field)
            level_copy(level + 1, piece).start()
            inputs[level + 1, piece, rows_at(bit), :] = rows_of(
                level, piece, rows_at(bit), field
            )
        else:
            final[piece] = rows_of(level, piece, slice(None), field)

    for step in range(pieces + levels - 1):
        for level in range(levels):
            piece = step - level
            if 0 <= piece < pieces:
                run_level(level, piece)

    for tile in range(pieces):
        low_piece, high_piece = [
            place if place < pieces else place - pieces for place in (2 * tile, 2 * tile + 1)
        ]
        out_ref[:, tile * LANES : (tile + 1) * LANES] = jnp.where(
            low_lanes, final[low_piece].astype(F32), final[high_piece].astype(F32)
        ).astype(BF16)

    for copy in small:
        copy.wait_send()
    for piece in range(pieces):
        side_copy(piece).wait_send()
        sibling_copy(piece, 0).wait_send()
        sibling_copy(piece, 1).wait_send()
        for level in range(1, levels):
            level_copy(level, piece).wait_send()


def body(sources, leaf_perm, leaf_factor, owner_map, coupling, transfer):
    height, width = sources.shape
    half = height // 2
    levels = transfer.shape[0]
    pieces = width // LANES
    assert width == pieces * LANES and pieces % 2 == 1
    vmem = pl.BlockSpec(memory_space=pltpu.VMEM)
    anywhere = pl.BlockSpec(memory_space=pl.ANY)
    dma = pltpu.SemaphoreType.DMA
    return pl.pallas_call(
        functools.partial(kernel, levels),
        out_shape=jax.ShapeDtypeStruct(sources.shape, sources.dtype),
        in_specs=[anywhere] * 6,
        out_specs=vmem,
        scratch_shapes=[
            pltpu.VMEM(leaf_perm.shape, leaf_perm.dtype),
            pltpu.VMEM(owner_map.shape, owner_map.dtype),
            pltpu.VMEM(coupling.shape, coupling.dtype),
            pltpu.VMEM(sources.shape, BF16),
            pltpu.VMEM(leaf_factor.shape, BF16),
            pltpu.VMEM(transfer.shape, BF16),
            pltpu.VMEM(leaf_factor.shape, BF16),
            pltpu.VMEM(leaf_factor.shape, BF16),
            pltpu.VMEM((pieces, half, LANES), BF16),
            pltpu.VMEM((pieces, height, LANES), BF16),
            pltpu.VMEM((pieces, height, LANES), BF16),
            pltpu.VMEM((levels, pieces, height, LANES), BF16),
            pltpu.VMEM((levels - 1, pieces, half, LANES), BF16),
            pltpu.VMEM((pieces, height, LANES), BF16),
            pltpu.VMEM(coupling.shape, coupling.dtype),
            pltpu.VMEM(owner_map.shape, owner_map.dtype),
            dma((5 + levels,)),
            dma((2,)),
            dma((2,)),
            dma((pieces,)),
            dma((pieces,)),
            dma((2, pieces)),
            dma((2, pieces)),
            dma((levels - 1, pieces)),
            dma((levels - 1, pieces)),
        ],
        compiler_params=pltpu.CompilerParams(collective_id=0, has_side_effects=True, vmem_limit_bytes=20 * 1024 * 1024),
        name="apply",
    )(*[pltpu.with_memory_space_constraint(x, pltpu.HBM) for x in (leaf_perm, owner_map, coupling, sources, leaf_factor, transfer)])


def solution(mesh):
    placed = (
        P(("leaf", "inner"), None),
        P(("leaf", "inner"), None),
        P(("leaf", "inner"), None),
        P(None, "inner"),
        P(None, ("leaf", "inner")),
        P(None, None, ("leaf", "inner"), None),
    )
    return jax.shard_map(
        body, mesh=mesh, in_specs=placed, out_specs=P(("leaf", "inner"), None), check_vma=False
    )
```

```python
import functools

import jax
import jax.numpy as jnp
from jax import lax
from jax.experimental import pallas as pl
from jax.experimental.pallas import tpu as pltpu
from jax.sharding import PartitionSpec as P

LANES = 128
PIECE = LANES // 2
MESH = pl.DeviceIdType.MESH
F32 = jnp.float32
BF16 = jnp.bfloat16


def dot(a, b):
    return jnp.dot(a, b, preferred_element_type=F32)


def as_column(row):
    return jnp.broadcast_to(row, (LANES, row.shape[1])).T


def kernel(
    levels,
    perm_hbm,
    owner_hbm,
    couple_hbm,
    source_hbm,
    factor_hbm,
    transfer_hbm,
    out_ref,
    perm_ref,
    owner_ref,
    couple_ref,
    source,
    factor,
    weights,
    lower_real,
    lower_imag,
    mine,
    prepared,
    theirs,
    inputs,
    outgoing,
    final,
    partner_couple,
    partner_owner,
    couple_real_cols,
    couple_imag_cols,
    owner_cols,
    load_sem,
    small_send,
    small_recv,
    side_send,
    side_recv,
    sib_send,
    sib_recv,
    level_send,
    level_recv,
):
    height, width = source.shape
    half = height // 2
    pieces = width // LANES
    leaf = lax.axis_index("leaf")
    inner = lax.axis_index("inner")
    inner_size = lax.axis_size("inner")
    sibling = leaf + 1 - 2 * lax.rem(leaf, 2)
    which_side = lax.rem(leaf, 2)
    pair = leaf // 2

    bits, partners = [], []
    for level in range(levels):
        distance = inner_size >> (level + 1)
        bit = lax.rem(inner // distance, 2)
        bits.append(bit)
        partners.append(inner + distance - 2 * distance * bit)

    def rows_at(flag):
        return pl.ds(pl.multiple_of(flag * half, half), half)

    barrier = pltpu.get_barrier_semaphore()
    pl.semaphore_signal(barrier, inc=1, device_id={"leaf": sibling}, device_id_type=MESH)
    for level in range(levels):
        pl.semaphore_signal(
            barrier, inc=1, device_id={"inner": partners[level]}, device_id_type=MESH
        )

    load_list = [
        (perm_hbm, perm_ref),
        (source_hbm, source),
        (factor_hbm, factor),
        (couple_hbm, couple_ref),
        (owner_hbm, owner_ref),
    ] + [(transfer_hbm.at[level], weights.at[level]) for level in range(levels)]
    loads = [
        pltpu.make_async_copy(origin, place, load_sem.at[number])
        for number, (origin, place) in enumerate(load_list)
    ]
    for load in loads:
        load.start()

    lane = lax.broadcasted_iota(jnp.int32, (height, LANES), 1)
    low_lanes = lane < PIECE
    sign_even = jnp.where(low_lanes, -1.0, 1.0).astype(F32)

    def turned(value, piece):
        rolled = pltpu.roll(value, PIECE, 1)
        sign = sign_even[: value.shape[0]]
        return rolled * sign if piece % 2 == 0 else rolled * -sign

    loads[0].wait()
    perm_column = as_column(perm_ref[...])
    one_hot = jnp.concatenate(
        [
            jnp.where(perm_column == lane + LANES * tile, 1.0, 0.0).astype(BF16)
            for tile in range(height // LANES)
        ],
        axis=1,
    )

    loads[2].wait()
    row_half = lax.broadcasted_iota(jnp.int32, (half, half), 0)
    col_half = lax.broadcasted_iota(jnp.int32, (half, half), 1)
    for part in range(2):
        here = slice(part * half, (part + 1) * half)
        block = factor[here, here].astype(F32)
        lower_real[here, here] = jnp.where(row_half >= col_half, block, 0.0).astype(BF16)
        lower_imag[here, here] = jnp.where(row_half > col_half, block.T, 0.0).astype(BF16)
    lower_real[half:, :half] = factor[half:, :half]
    lower_imag[half:, :half] = factor[:half, half:].astype(F32).T.astype(BF16)

    loads[1].wait()
    loads[3].wait()
    loads[4].wait()

    small = [
        pltpu.make_async_remote_copy(
            src_ref=couple_ref,
            dst_ref=partner_couple,
            send_sem=small_send.at[0],
            recv_sem=small_recv.at[0],
            device_id={"inner": partners[0]},
            device_id_type=MESH,
        ),
        pltpu.make_async_remote_copy(
            src_ref=owner_ref,
            dst_ref=partner_owner,
            send_sem=small_send.at[1],
            recv_sem=small_recv.at[1],
            device_id={"inner": partners[0]},
            device_id_type=MESH,
        ),
    ]
    kept, other = rows_at(bits[0]), rows_at(1 - bits[0])

    def side_copy(piece):
        return pltpu.make_async_remote_copy(
            src_ref=mine.at[piece],
            dst_ref=prepared.at[piece, kept],
            send_sem=side_send.at[piece],
            recv_sem=side_recv.at[piece],
            device_id={"inner": partners[0]},
            device_id_type=MESH,
        )

    def sibling_copy(piece, stage):
        rows = kept if stage == 0 else other
        return pltpu.make_async_remote_copy(
            src_ref=prepared.at[piece, rows],
            dst_ref=theirs.at[piece, rows],
            send_sem=sib_send.at[stage, piece],
            recv_sem=sib_recv.at[stage, piece],
            device_id={"leaf": sibling},
            device_id_type=MESH,
        )

    def level_copy(level, piece):
        return pltpu.make_async_remote_copy(
            src_ref=outgoing.at[level - 1, piece],
            dst_ref=inputs.at[level, piece, rows_at(bits[level])],
            send_sem=level_send.at[level - 1, piece],
            recv_sem=level_recv.at[level - 1, piece],
            device_id={"inner": partners[level]},
            device_id_type=MESH,
        )

    def prepare(piece):
        real_tile, imag_tile = piece // 2, (pieces + piece) // 2
        low_tile, high_tile = (
            (real_tile, imag_tile) if piece % 2 == 0 else (imag_tile, real_tile)
        )
        column = jnp.where(
            low_lanes,
            source[:, low_tile * LANES : (low_tile + 1) * LANES].astype(F32),
            source[:, high_tile * LANES : (high_tile + 1) * LANES].astype(F32),
        ).astype(BF16)
        permuted = dot(one_hot, column)
        permuted_half = permuted.astype(BF16)
        results = []
        for part in range(2):
            here = slice(part * half, (part + 1) * half)
            depth = (part + 1) * half
            real_part = dot(lower_real[here, :depth], permuted_half[:depth])
            imag_part = dot(lower_imag[here, :depth], permuted_half[:depth])
            results.append(
                (permuted[here] + real_part + turned(imag_part, piece)).astype(BF16)
            )
        top, bottom = results
        upper = bits[0] == 1
        prepared[piece, kept, :] = jnp.where(upper, bottom, top)
        mine[piece] = jnp.where(upper, top, bottom)
        if piece == 0:
            pl.semaphore_wait(barrier, levels + 1)
        sibling_copy(piece, 0).start()
        side_copy(piece).start()
        if piece == 0:
            for copy in small:
                copy.start()

    def forward(piece):
        side_copy(piece).wait_recv()
        sibling_copy(piece, 1).start()

    lag = 5
    for piece in range(pieces):
        prepare(piece)
        if piece >= lag:
            forward(piece - lag)

    for copy in small:
        copy.wait_recv()

    def in_input_order(own, partner):
        low, high = slice(0, half), slice(half, height)
        return jnp.concatenate(
            [
                jnp.where(bits[0] == 0, own[:, low], partner[:, high]),
                jnp.where(bits[0] == 1, own[:, high], partner[:, low]),
            ],
            axis=1,
        )

    couple_rows = in_input_order(couple_ref[...], partner_couple[...])
    owner_rows = in_input_order(
        owner_ref[pl.ds(pair, 1), :], partner_owner[pl.ds(pair, 1), :]
    )
    couple_real = as_column(couple_rows[0:1])
    couple_imag = as_column(couple_rows[1:2])
    own_first_column = as_column(owner_rows)

    for piece in range(pieces - lag, pieces):
        forward(piece)

    scratch_rows = [couple_real_cols, couple_imag_cols, owner_cols]
    for place, column in zip(scratch_rows, (couple_real, couple_imag, own_first_column)):
        place[...] = column

    def combine(piece, rows):
        here = prepared[piece, rows, :].astype(F32)
        there = theirs[piece, rows, :].astype(F32)
        own_first = owner_cols[rows, :] == which_side
        first_part = jnp.where(own_first, here, there)
        other_part = jnp.where(own_first, there, here)
        return (
            first_part
            + couple_real_cols[rows, :] * other_part
            + couple_imag_cols[rows, :] * turned(other_part, piece)
        ).astype(BF16)

    def products(level, rows, cols, field):
        return (
            dot(weights[level, 0, rows, cols], field),
            dot(weights[level, 1, rows, cols], field),
        )

    def rounded(parts, piece):
        return (parts[0] + turned(parts[1], piece)).astype(BF16)

    loaded = set()
    done = set()

    def finish(tile):
        low_piece, high_piece = sources_of(tile)
        out_ref[:, tile * LANES : (tile + 1) * LANES] = jnp.where(
            low_lanes, final[low_piece].astype(F32), final[high_piece].astype(F32)
        ).astype(BF16)

    def sources_of(tile):
        return [
            place if place < pieces else place - pieces for place in (2 * tile, 2 * tile + 1)
        ]

    def run_level(level, piece):
        kept_here, other_here = rows_at(bits[level]), rows_at(1 - bits[level])
        if level not in loaded:
            loads[5 + level].wait()
            loaded.add(level)
        if level + 1 < levels:
            bit = bits[level + 1]
            order = [rows_at(1 - bit), rows_at(bit)]
        else:
            order = [slice(0, half), slice(half, height)]
        if level == 0:
            sibling_copy(piece, 0).wait_recv()
            own_field = combine(piece, kept_here)
        else:
            own_field = inputs[level, piece, kept_here, :]
        early = piece in early_pieces
        if early:
            own_parts = [products(level, rows, kept_here, own_field) for rows in order]
        if level == 0:
            sibling_copy(piece, 1).wait_recv()
            partner_field = combine(piece, other_here)
        else:
            level_copy(level, piece).wait_recv()
            partner_field = inputs[level, piece, other_here, :]
        if not early:
            if level == 0:
                inputs[0, piece, kept_here, :] = own_field
                inputs[0, piece, other_here, :] = partner_field
            field = inputs[level, piece]
        for place, rows in enumerate(order):
            if early:
                partner_parts = products(level, rows, other_here, partner_field)
                parts = [a + b for a, b in zip(own_parts[place], partner_parts)]
            else:
                parts = products(level, rows, slice(None), field)
            value = rounded(parts, piece)
            if level + 1 == levels:
                final[piece, rows, :] = value
            elif place == 0:
                outgoing[level, piece] = value
                level_copy(level + 1, piece).start()
            else:
                inputs[level + 1, piece, rows, :] = value
        if level + 1 == levels:
            done.add(piece)
            for tile in range(pieces):
                if piece in sources_of(tile) and done.issuperset(sources_of(tile)):
                    finish(tile)

    early_pieces = {pieces - 1}
    for step in range(pieces + 2 * levels):
        for level in range(levels):
            piece = step - (level + (level > 0))
            if 0 <= piece < pieces:
                run_level(level, piece)

    for copy in small:
        copy.wait_send()
    for piece in range(pieces):
        side_copy(piece).wait_send()
        sibling_copy(piece, 0).wait_send()
        sibling_copy(piece, 1).wait_send()
        for level in range(1, levels):
            level_copy(level, piece).wait_send()


def body(sources, leaf_perm, leaf_factor, owner_map, coupling, transfer):
    height, width = sources.shape
    half = height // 2
    levels = transfer.shape[0]
    pieces = width // LANES
    assert width == pieces * LANES and pieces % 2 == 1
    vmem = pl.BlockSpec(memory_space=pltpu.VMEM)
    anywhere = pl.BlockSpec(memory_space=pl.ANY)
    dma = pltpu.SemaphoreType.DMA
    return pl.pallas_call(
        functools.partial(kernel, levels),
        out_shape=jax.ShapeDtypeStruct(sources.shape, sources.dtype),
        in_specs=[anywhere] * 6,
        out_specs=vmem,
        scratch_shapes=[
            pltpu.VMEM(leaf_perm.shape, leaf_perm.dtype),
            pltpu.VMEM(owner_map.shape, owner_map.dtype),
            pltpu.VMEM(coupling.shape, coupling.dtype),
            pltpu.VMEM(sources.shape, BF16),
            pltpu.VMEM(leaf_factor.shape, BF16),
            pltpu.VMEM(transfer.shape, BF16),
            pltpu.VMEM(leaf_factor.shape, BF16),
            pltpu.VMEM(leaf_factor.shape, BF16),
            pltpu.VMEM((pieces, half, LANES), BF16),
            pltpu.VMEM((pieces, height, LANES), BF16),
            pltpu.VMEM((pieces, height, LANES), BF16),
            pltpu.VMEM((levels, pieces, height, LANES), BF16),
            pltpu.VMEM((levels - 1, pieces, half, LANES), BF16),
            pltpu.VMEM((pieces, height, LANES), BF16),
            pltpu.VMEM(coupling.shape, coupling.dtype),
            pltpu.VMEM(owner_map.shape, owner_map.dtype),
            pltpu.VMEM((height, LANES), coupling.dtype),
            pltpu.VMEM((height, LANES), coupling.dtype),
            pltpu.VMEM((height, LANES), owner_map.dtype),
            dma((5 + levels,)),
            dma((2,)),
            dma((2,)),
            dma((pieces,)),
            dma((pieces,)),
            dma((2, pieces)),
            dma((2, pieces)),
            dma((levels - 1, pieces)),
            dma((levels - 1, pieces)),
        ],
        compiler_params=pltpu.CompilerParams(collective_id=0, has_side_effects=True, vmem_limit_bytes=20 * 1024 * 1024),
        name="apply",
    )(*[pltpu.with_memory_space_constraint(x, pltpu.HBM) for x in (leaf_perm, owner_map, coupling, sources, leaf_factor, transfer)])


def solution(mesh):
    placed = (
        P(("leaf", "inner"), None),
        P(("leaf", "inner"), None),
        P(("leaf", "inner"), None),
        P(None, "inner"),
        P(None, ("leaf", "inner")),
        P(None, None, ("leaf", "inner"), None),
    )
    return jax.shard_map(
        body, mesh=mesh, in_specs=placed, out_specs=P(("leaf", "inner"), None), check_vma=False
    )
```
